512 devices in a mesh: leaf: 4 (over y), row: 4 (over x), col: 32 (over z, core).
Axes of the slice: x: 4, y: 4, z: 16, core: 2. Of those that a mesh axis runs over, the one named last changes fastest.
Arguments:
- fronts: float32 [4, 8192, 8192], P('leaf', 'row', 'col'), as said below
- row_targets: int32 [4, 8192], P('leaf', 'row'), may hold values from -1 to 8191, as said below
- col_targets: int32 [4, 8192], P('leaf', 'col'), may hold values from -1 to 8191, as said below
Outputs:
- factored: float32 [4, 8192, 8192], P('leaf', 'row', 'col')
- parent: float32 [8192, 8192], P(('leaf', 'row'), 'col')
The draws below stay inside these ranges and needn't reach their ends.
Inputs may be any that keep to these rules, and one draw needn't show every extreme that they name: `fronts`: each front is symmetric and positive definite; in group g the rows and columns from some index of at least 6272 on are those of the identity. `row_targets`: for each group: -1 on the first 512 indices and on the identity rows of its front, 0 or more elsewhere; the non-negative entries of one group are distinct; among one group's entries in an aligned block of 2048 indices at most 128 lie in any one aligned block of 512 parent rows, and one such parent block, the same for every group and block, receives exactly 128 from each. `col_targets`: -1 exactly where row_targets is -1; every other entry lies in the same aligned block of 256 as its own index, and the entries of one group are distinct.
All inputs are finite; a program needn't handle non-finite values.
Results may differ from the reference program's by a relative error of at most 0.0001.
Values sent between devices are 32-bit elements; how exact they have to be, the bound alone decides.
No kernel may reach another device: no remote copies, remote signals or barrier semaphores. Data moves between devices by JAX's collectives and lax.ppermute only.
A program may use at most 64 MiB of HBM per device.

```python
import math
import jax
import jax.numpy as jnp
from jax import lax

W = 256
PANELS = 2
M = 8192
ROWBLK = 2048
COLBLK = 256
PARBLK = 512
CAPACITY = 128
PIVOTS = 512
N_LEAF = 4
N_ROW = 4
N_COL = 32


def shuffle_rows(key_list, length):

    def single(one_key):
        return jax.random.permutation(one_key, length).astype(jnp.int32)
    return jax.vmap(single)(key_list)


def group_layout(key, group_id):
    favored = jax.random.randint(jax.random.fold_in(key, 17), (), 0, N_LEAF * N_ROW)
    group_key = jax.random.fold_in(key, 1000 + group_id)
    ending = jax.random.randint(jax.random.fold_in(group_key, 1), (), M - ROWBLK + CAPACITY, M + 1)
    positions = jnp.arange(M, dtype=jnp.int32)
    is_live = (positions >= PIVOTS) & (positions < ending)
    ranks = jnp.cumsum(is_live.reshape(N_ROW, ROWBLK).astype(jnp.int32), axis=1) - 1
    shuffled = shuffle_rows(jax.random.split(jax.random.fold_in(group_key, 2), N_ROW), ROWBLK)
    later = jnp.where(shuffled // CAPACITY == favored, 0, 1).astype(jnp.int32)
    ordering = jnp.argsort(later, axis=1, stable=True)
    slot_order = jnp.take_along_axis(shuffled, ordering, axis=1)
    chosen = jnp.take_along_axis(slot_order, jnp.clip(ranks, 0, ROWBLK - 1), axis=1)
    owner_ids = chosen // CAPACITY
    within = chosen % CAPACITY + jnp.arange(N_ROW, dtype=jnp.int32)[:, None] * CAPACITY
    spots = shuffle_rows(jax.random.split(jax.random.fold_in(group_key, 3), N_LEAF * N_ROW), PARBLK)
    row_place = owner_ids * PARBLK + spots[owner_ids, within]
    row_list = jnp.where(is_live, row_place.reshape(M), -1).astype(jnp.int32)
    col_perm = shuffle_rows(jax.random.split(jax.random.fold_in(group_key, 4), N_COL), COLBLK)
    col_place = jnp.arange(N_COL, dtype=jnp.int32)[:, None] * COLBLK + col_perm
    col_list = jnp.where(is_live, col_place.reshape(M), -1).astype(jnp.int32)
    return (group_key, ending, row_list, col_list)


def group_matrix(key, group_id):
    group_key, ending, row_list, col_list = group_layout(key, group_id)
    positions = jnp.arange(M, dtype=jnp.int32)
    noise = jax.random.uniform(jax.random.fold_in(group_key, 5), (M, M), jnp.float32, -1.5, 1.5) * (1.0 / math.sqrt(M))
    symmetric = (noise + noise.T) * 0.70710678
    diag_values = jax.random.uniform(jax.random.fold_in(group_key, 6), (M,), jnp.float32, 2.5, 4.5)
    padding = positions >= ending
    offdiag = jnp.where(padding[:, None] | padding[None, :], 0.0, symmetric)
    diag_full = jnp.where(padding, 1.0, diag_values)
    same_index = positions[:, None] == positions[None, :]
    return jnp.where(same_index, diag_full[:, None], offdiag).astype(jnp.float32)


def draw_fronts(key, part):
    return jnp.stack([group_matrix(key, group_id) for group_id in range(N_LEAF)])


def draw_row_targets(key, part):
    return jnp.stack([group_layout(key, group_id)[2] for group_id in range(N_LEAF)])


def draw_col_targets(key, part):
    return jnp.stack([group_layout(key, group_id)[3] for group_id in range(N_LEAF)])


def setup_inputs(seed: int = 0) -> dict:
    seeds = jax.random.split(jax.random.key(seed), 4)
    fronts = draw_fronts(jax.random.fold_in(seeds[3], 71), 0)
    row_targets = draw_row_targets(jax.random.fold_in(seeds[3], 71), 0)
    col_targets = draw_col_targets(jax.random.fold_in(seeds[3], 71), 0)
    return {"fronts": fronts, "row_targets": row_targets, "col_targets": col_targets}


def factor_front(matrix):
    positions = jnp.arange(matrix.shape[0])
    for step_index in range(PANELS):
        first_col = step_index * W
        after_col = first_col + W
        lower_factor = jnp.linalg.cholesky(matrix[first_col:after_col, first_col:after_col])
        solved = jax.scipy.linalg.solve_triangular(lower_factor, matrix[:, first_col:after_col].T, lower=True).T
        masked = jnp.where((positions >= after_col)[:, None], solved, jnp.float32(0.0))
        matrix = matrix - jnp.dot(masked, masked.T, precision=lax.Precision.HIGHEST)
        column = masked.at[first_col:after_col].set(lower_factor)
        matrix = matrix.at[:, first_col:after_col].set(column)
    return matrix

def place_group(factor_matrix, row_list, col_list):
    total = factor_matrix.shape[0]
    row_safe = jnp.where(row_list >= 0, row_list, total)
    col_safe = jnp.where(col_list >= 0, col_list, total)
    by_rows = jnp.zeros_like(factor_matrix).at[row_safe].add(factor_matrix, mode='drop')
    return jnp.zeros_like(factor_matrix).at[:, col_safe].add(by_rows, mode='drop')

def reference(fronts, row_targets, col_targets):
    results = []
    parent = jnp.zeros(fronts.shape[1:], jnp.float32)
    for group_id in range(fronts.shape[0]):
        done = factor_front(fronts[group_id])
        results.append(done)
        parent = parent + place_group(done, row_targets[group_id], col_targets[group_id])
    return (jnp.stack(results), parent)
```

```python
import jax
import jax.numpy as jnp
from jax import lax
from jax.experimental import pallas as pl
from jax.experimental.pallas import tpu as pltpu
from jax.sharding import PartitionSpec as P

W = 256
PIV = 512
NB = 128
HIGHEST = lax.Precision.HIGHEST
GRID = ("row", "col")


def dot_f32(a, b, dims=((1,), (0,))):
    return lax.dot_general(
        a, b, (dims, ((), ())), precision=HIGHEST, preferred_element_type=jnp.float32
    )


def split(x):
    high = x.astype(jnp.bfloat16)
    low = (x - high.astype(jnp.float32)).astype(jnp.bfloat16)
    return high, low


def factor_block(block):
    groups = NB // 8
    sub = lax.broadcasted_iota(jnp.int32, (8, NB), 0)
    lane = lax.broadcasted_iota(jnp.int32, (8, NB), 1)
    mat = [block[8 * i : 8 * i + 8, :] for i in range(groups)]
    inv = [jnp.where(lane == sub + 8 * i, 1.0, 0.0).astype(jnp.float32) for i in range(groups)]
    for j in range(NB):
        g, k = divmod(j, 8)
        cols = [jnp.broadcast_to(mat[i][:, j : j + 1], (8, NB)) for i in range(g, groups)]
        pivot = jnp.broadcast_to(cols[0][k : k + 1, :], (8, NB))
        recip = 1.0 / pivot
        row_m = jnp.broadcast_to(mat[g][k : k + 1, :], (8, NB)) * recip
        row_i = jnp.broadcast_to(inv[g][k : k + 1, :], (8, NB)) * recip
        cols[0] = jnp.where(sub > k, cols[0], 0.0)
        for i in range(g, groups):
            mat[i] = mat[i] - cols[i - g] * row_m
            inv[i] = inv[i] - cols[i - g] * row_i
    upper, lower_inv = [], []
    for i in range(groups):
        on_diag = lane == sub + 8 * i
        diag = jnp.sum(jnp.where(on_diag, mat[i], 0.0), axis=1, keepdims=True)
        scale = 1.0 / jnp.sqrt(diag)
        upper.append(jnp.where(lane >= sub + 8 * i, mat[i] * scale, 0.0))
        lower_inv.append(inv[i] * scale)
    return jnp.concatenate(upper, axis=0), jnp.concatenate(lower_inv, axis=0)


def factor_kernel(place, left, right, mine, z_ref, top_ref, work, low, low_inv):
    work[:, 0:W] = left[...]
    work[:, W:PIV] = right[...]
    low[...] = jnp.zeros_like(low)
    low_inv[...] = jnp.zeros_like(low_inv)
    rows = lax.broadcasted_iota(jnp.int32, (PIV, NB), 0)
    for k in range(PIV // NB):
        at = slice(k * NB, (k + 1) * NB)
        upper, inverse = factor_block(work[at, at])
        column = dot_f32(work[:, at], inverse, ((1,), (1,)))
        column = jnp.where(rows >= (k + 1) * NB, column, 0.0)
        if k + 1 < PIV // NB:
            after = slice((k + 1) * NB, PIV)
            below = column[(k + 1) * NB :, :]
            work[after, after] = work[after, after] - dot_f32(below, below, ((1,), (1,)))
        if k:
            carried = dot_f32(low[at, 0 : k * NB], low_inv[0 : k * NB, 0 : k * NB])
            low_inv[at, 0 : k * NB] = -dot_f32(inverse, carried)
        low_inv[at, at] = inverse
        low[:, at] = column
        low[at, at] = upper.T
    col = place[1]
    own = mine[...]
    solved = dot_f32(low_inv[...], own)
    unit_row = lax.broadcasted_iota(jnp.int32, (PIV, W), 0)
    unit_col = lax.broadcasted_iota(jnp.int32, (PIV, W), 1)
    unit = jnp.where(unit_row == unit_col + col * W, -1.0, 0.0)
    chosen = jnp.where(col < PIV // W, unit, solved)
    z_ref[...] = dot_f32(low_inv[...], chosen, ((0,), (0,)))
    top_ref[0:W, :] = own[0:W, :]
    top_ref[W:PIV, :] = own[W:PIV, :] - dot_f32(low[W:PIV, 0:W], solved[0:W, :])

    @pl.when(col == 0)
    def _():
        top_ref[...] = low[:, 0:W]

    @pl.when(col == 1)
    def _():
        top_ref[...] = low[:, W:PIV]


def update_kernel(place, front, panel, z_ref, top, col_place, slot, out_ref, send_ref, pair):
    row, col = place[0], place[1]
    keep = jnp.where(col < PIV // W, 0.0, 1.0)
    weights = []
    for a in range(4):
        start = pl.multiple_of(((a - row) & 3) * NB, NB)
        weights.append(z_ref[pl.ds(start, NB), :])
    z_all = jnp.concatenate(weights, axis=0)
    for b in range(8):
        at = slice(b * W, (b + 1) * W)
        lhs = jnp.concatenate([panel[8 * a + b] for a in range(4)], axis=0)
        value = front[at, :] * keep - dot_f32(lhs, z_all, ((0,), (0,)))
        out_ref[at, :] = value

    @pl.when(row == 0)
    def _():
        out_ref[0:PIV, :] = top[...]

    for b in range(8):
        at = slice(b * W, (b + 1) * W)
        high, low = split(out_ref[at, :])
        pair[at, 0:W] = jnp.dot(high, col_place[...], preferred_element_type=jnp.float32).astype(jnp.bfloat16)
        pair[at, W : 2 * W] = jnp.dot(low, col_place[...], preferred_element_type=jnp.float32).astype(jnp.bfloat16)
    for b in range(4):
        want = lax.broadcasted_iota(jnp.int32, (512, 2048), 0) + b * 512
        hit = jnp.where(slot[...] == want, 1.0, 0.0).astype(jnp.bfloat16)
        both = jnp.dot(hit, pair[...], preferred_element_type=jnp.float32)
        send_ref[b * 512 : (b + 1) * 512, :] = both[:, 0:W] + both[:, W : 2 * W]


def place_kernel(select, values, out_ref):
    high, low = split(values[...])
    out_ref[...] = jnp.dot(select[...], high, preferred_element_type=jnp.float32) + jnp.dot(
        select[...], low, preferred_element_type=jnp.float32
    )


SMEM = pl.BlockSpec(memory_space=pltpu.SMEM)
VMEM = pl.BlockSpec(memory_space=pltpu.VMEM)
PARAMS = pltpu.CompilerParams(vmem_limit_bytes=56 << 20)


def cost(flops, moved):
    return pl.CostEstimate(flops=flops, bytes_accessed=moved, transcendentals=0)


def shards(fronts, row_targets, col_targets):
    f32 = jnp.float32
    front = fronts[0]
    rows_here, cols_here = front.shape
    row = lax.axis_index("row")
    col = lax.axis_index("col")
    place = jnp.stack([row, col]).astype(jnp.int32)
    head = front[0:PIV, :]

    shares = [
        lax.ppermute(
            head[j * NB : (j + 1) * NB],
            GRID,
            [(8 * r + b, r * 32 + 8 * ((r + j) % 4) + b) for r in range(4) for b in range(8)],
        )
        for j in range(4)
    ]
    share = shares[0] + shares[1] + shares[2] + shares[3]
    panel = lax.all_gather(share, "col")

    piece = lax.all_to_all(head.reshape(4, NB, W), "row", 0, 0, tiled=True)[0]
    piece = jnp.where(col < 2, piece, 0.0)
    first = [lax.ppermute(piece, "col", [(q, q + 8 * j) for q in range(2)]) for j in range(1, 4)]
    piece = piece + (first[0] + first[1]) + first[2]
    second = [
        lax.ppermute(piece, "col", [(8 * a + q, 8 * a + q + 2 * j) for a in range(4) for q in range(2)])
        for j in range(1, 4)
    ]
    piece = piece + (second[0] + second[1]) + second[2]
    half = lax.all_gather(piece, "row", tiled=True)
    other = lax.ppermute(half, "col", [(i, i ^ 1) for i in range(32)])
    even = (col % 2) == 0
    left = jnp.where(even, half, other)
    right = jnp.where(even, other, half)

    spread = [lax.ppermute(head, "row", [(0, j)]) for j in range(1, 4)]
    mine = jnp.where(row == 0, head, spread[0] + spread[1] + spread[2])

    z_all, top = pl.pallas_call(
        factor_kernel,
        out_shape=[jax.ShapeDtypeStruct((PIV, W), f32)] * 2,
        in_specs=[SMEM, VMEM, VMEM, VMEM],
        out_specs=[VMEM, VMEM],
        scratch_shapes=[pltpu.VMEM((PIV, PIV), f32)] * 3,
        compiler_params=PARAMS,
        cost_estimate=cost(40_000_000_000, 4 << 20),
    )(place, left, right, mine)

    local_cols = col_targets[0] - col * cols_here
    col_place = (local_cols[:, None] == jnp.arange(cols_here, dtype=jnp.int32)[None, :]).astype(jnp.bfloat16)
    targets = row_targets[0]
    live = targets >= 0
    owners = jnp.where(live, targets // 512, -1)
    hits = owners[:, None] == jnp.arange(16, dtype=jnp.int32)[None, :]
    index = jnp.arange(rows_here, dtype=jnp.int32)
    before = (index[:, None] > index[None, :]).astype(jnp.bfloat16)
    ranks = jnp.dot(before, hits.astype(jnp.bfloat16), preferred_element_type=f32)
    rank = jnp.sum(jnp.where(hits, ranks, 0.0), axis=1).astype(jnp.int32)
    slot = jnp.where(live, owners * 128 + rank, -1)
    offset = jnp.where(live, targets % 512 + 1, 0)
    digits = jnp.stack([offset // 16, offset % 16], axis=1).astype(jnp.bfloat16)
    at_slot = (index[:, None] == slot[None, :]).astype(jnp.bfloat16)
    found = jnp.dot(at_slot, digits, preferred_element_type=f32)
    offsets = (found[:, 0] * 16.0 + found[:, 1]).astype(jnp.int32) - 1
    offsets_in = lax.all_to_all(offsets.reshape(16, 1, 128), ("leaf", "row"), 0, 0, tiled=True).reshape(-1)
    select = (jnp.arange(512, dtype=jnp.int32)[:, None] == offsets_in[None, :]).astype(jnp.bfloat16)

    out, send = pl.pallas_call(
        update_kernel,
        out_shape=[jax.ShapeDtypeStruct((rows_here, cols_here), f32)] * 2,
        in_specs=[SMEM] + [VMEM] * 6,
        out_specs=[VMEM, VMEM],
        scratch_shapes=[pltpu.VMEM((rows_here, 2 * cols_here), jnp.bfloat16)],
        compiler_params=PARAMS,
        cost_estimate=cost(6_000_000_000, 12 << 20),
    )(place, front, panel, z_all, top, col_place, slot.reshape(1, rows_here))

    received = lax.all_to_all(send.reshape(16, 128, cols_here), ("leaf", "row"), 0, 0, tiled=True)
    parent = pl.pallas_call(
        place_kernel,
        out_shape=jax.ShapeDtypeStruct((512, cols_here), f32),
        in_specs=[VMEM, VMEM],
        out_specs=VMEM,
        compiler_params=PARAMS,
        cost_estimate=cost(1_000_000_000, 5 << 20),
    )(select, received.reshape(2048, cols_here))
    return (out[None], parent)


def solution(mesh):
    placed = (P("leaf", "row", "col"), P("leaf", "row"), P("leaf", "col"))
    return jax.shard_map(
        shards,
        mesh=mesh,
        in_specs=placed,
        out_specs=(P("leaf", "row", "col"), P(("leaf", "row"), "col")),
        check_vma=False,
    )
```

```python
import jax
import jax.numpy as jnp
from jax import lax
from jax.experimental import pallas as pl
from jax.experimental.pallas import tpu as pltpu
from jax.sharding import PartitionSpec as P

W = 256
PIV = 512
NB = 128
HIGHEST = lax.Precision.HIGHEST
GRID = ("row", "col")
SHARE_CHIP = ((0, -1, -2, -3), (1, -4, -5, -6), (2, 7, 8, 9), (3, 4, 5, 6))

def dot_f32(a, b, dims=((1,), (0,))):
    return lax.dot_general(
        a, b, (dims, ((), ())), precision=HIGHEST, preferred_element_type=jnp.float32
    )


def split(x):
    high = x.astype(jnp.bfloat16)
    low = (x - high.astype(jnp.float32)).astype(jnp.bfloat16)
    return high, low


def factor_block(block):
    groups = NB // 8
    sub = lax.broadcasted_iota(jnp.int32, (8, NB), 0)
    lane = lax.broadcasted_iota(jnp.int32, (8, NB), 1)
    mat = [block[8 * i : 8 * i + 8, :] for i in range(groups)]
    inv = [jnp.where(lane == sub + 8 * i, 1.0, 0.0).astype(jnp.float32) for i in range(groups)]
    full = (8, NB)
    for g in range(groups):
        own = [jnp.broadcast_to(mat[g][:, 8 * g + k : 8 * g + k + 1], full) for k in range(8)]
        part = [[jnp.broadcast_to(own[b][a : a + 1, :], full) for b in range(a + 1)] for a in range(8)]
        recip, unit = [], [[None] * 8 for _ in range(8)]
        for k in range(8):
            recip.append(1.0 / part[k][k])
            for a in range(k + 1, 8):
                unit[a][k] = part[a][k] * recip[k]
            for a in range(k + 1, 8):
                for b in range(k + 1, a + 1):
                    part[a][b] = part[a][b] - unit[a][k] * part[b][k]
        row_m = [jnp.broadcast_to(mat[g][k : k + 1, :], full) for k in range(8)]
        row_i = [jnp.broadcast_to(inv[g][k : k + 1, :], full) for k in range(8)]
        for k in range(8):
            for m in range(k):
                row_m[k] = row_m[k] - unit[k][m] * row_m[m]
                row_i[k] = row_i[k] - unit[k][m] * row_i[m]
        new_m, new_i = row_m[0], row_i[0]
        for k in range(1, 8):
            new_m = jnp.where(sub == k, row_m[k], new_m)
            new_i = jnp.where(sub == k, row_i[k], new_i)
        mat[g], inv[g] = new_m, new_i
        row_m = [row_m[k] * recip[k] for k in range(8)]
        row_i = [row_i[k] * recip[k] for k in range(8)]
        for i in range(g + 1, groups):
            cols = [jnp.broadcast_to(mat[i][:, 8 * g + k : 8 * g + k + 1], full) for k in range(8)]
            for k in range(8):
                for m in range(k):
                    cols[k] = cols[k] - unit[k][m] * cols[m]
                mat[i] = mat[i] - cols[k] * row_m[k]
                inv[i] = inv[i] - cols[k] * row_i[k]
    upper, lower_inv = [], []
    for i in range(groups):
        on_diag = lane == sub + 8 * i
        diag = jnp.sum(jnp.where(on_diag, mat[i], 0.0), axis=1, keepdims=True)
        scale = 1.0 / jnp.sqrt(diag)
        upper.append(jnp.where(lane >= sub + 8 * i, mat[i] * scale, 0.0))
        lower_inv.append(inv[i] * scale)
    return jnp.concatenate(upper, axis=0), jnp.concatenate(lower_inv, axis=0)


def share_kernel(a, b, c, d, out_ref):
    out_ref[...] = ((a[...] + b[...]) + (c[...] + d[...])).T


def factor_two(work, low, inverse):
    first, second = slice(0, NB), slice(NB, W)
    upper, inv_a = factor_block(work[first, first])
    below = dot_f32(work[second, first], inv_a, ((1,), (1,)))
    rest = work[second, second] - dot_f32(below, below, ((1,), (1,)))
    low[first, first] = upper.T
    low[second, first] = below
    low[first, second] = jnp.zeros((NB, NB), jnp.float32)
    upper, inv_b = factor_block(rest)
    low[second, second] = upper.T
    inverse[first, first] = inv_a
    inverse[first, second] = jnp.zeros((NB, NB), jnp.float32)
    inverse[second, second] = inv_b
    inverse[second, first] = -dot_f32(inv_b, dot_f32(below, inv_a))


def factor_first(block, under, last, low, inverse, low_under, rest):
    factor_two(block, low, inverse)
    below = dot_f32(under[...], inverse[...], ((1,), (1,)))
    low_under[...] = below
    rest[...] = last[...] - dot_f32(below, below, ((1,), (1,)))


def factor_second(block, low, inverse):
    factor_two(block, low, inverse)


def solve_kernel(place, low_a, inv_a, low_under, low_b, inv_b, mine, z_ref, top_ref):
    col = place[1]
    own_a, own_b = mine[0:W, :], mine[W:PIV, :]
    solved_a = dot_f32(inv_a[...], own_a)
    second = own_b - dot_f32(low_under[...], solved_a)
    solved_b = dot_f32(inv_b[...], second)
    unit_row = lax.broadcasted_iota(jnp.int32, (W, W), 0)
    unit_col = lax.broadcasted_iota(jnp.int32, (W, W), 1)
    unit = jnp.where(unit_row == unit_col, -1.0, 0.0)
    zero = jnp.zeros((W, W), jnp.float32)
    chosen_a = jnp.where(col == 0, unit, jnp.where(col == 1, zero, solved_a))
    chosen_b = jnp.where(col == 1, unit, jnp.where(col == 0, zero, solved_b))
    z_b = dot_f32(inv_b[...], chosen_b, ((0,), (0,)))
    z_ref[W:PIV, :] = z_b
    z_ref[0:W, :] = dot_f32(inv_a[...], chosen_a - dot_f32(low_under[...], z_b, ((0,), (0,))), ((0,), (0,)))
    top_ref[0:W, :] = jnp.where(col == 0, low_a[...], jnp.where(col == 1, zero, own_a))
    top_ref[W:PIV, :] = jnp.where(col == 0, low_under[...], jnp.where(col == 1, low_b[...], second))


def update_kernel(place, front, panel, z_ref, top, col_place, slot, out_ref, send_ref, pair):
    row, col = place[0], place[1]
    keep = jnp.where(col < PIV // W, 0.0, 1.0)
    for b in range(8):
        at = slice(b * W, (b + 1) * W)
        parts = []
        for k in range(4):
            parts.append(panel[2 * ((4 * row + SHARE_CHIP[b // 2][k]) & 15) + b % 2])
        rows = jnp.concatenate(parts, axis=1)
        value = front[at, :] * keep - dot_f32(rows, z_ref[...])
        if b < PIV // W:
            value = jnp.where(row == 0, top[at, :], value)
        out_ref[at, :] = value
        for part, piece in enumerate(split(value)):
            moved = jnp.dot(piece, col_place[...], preferred_element_type=jnp.float32)
            pair[at, part * W : (part + 1) * W] = moved.astype(jnp.bfloat16)
    for b in range(4):
        want = lax.broadcasted_iota(jnp.int32, (512, 2048), 0) + b * 512
        hit = jnp.where(slot[...] == want, 1.0, 0.0).astype(jnp.bfloat16)
        both = jnp.dot(hit, pair[...], preferred_element_type=jnp.float32)
        send_ref[b * 512 : (b + 1) * 512, :] = both[:, 0:W] + both[:, W : 2 * W]


def place_kernel(select, values, out_ref):
    high, low = split(values[...])
    out_ref[...] = jnp.dot(select[...], high, preferred_element_type=jnp.float32) + jnp.dot(
        select[...], low, preferred_element_type=jnp.float32
    )


SMEM = pl.BlockSpec(memory_space=pltpu.SMEM)
VMEM = pl.BlockSpec(memory_space=pltpu.VMEM)
F32 = jnp.float32


def call(body, ins, outs, flops, limit, scratch=(), scalars=0):
    return pl.pallas_call(
        body,
        out_shape=outs,
        in_specs=[SMEM] * scalars + [VMEM] * (ins - scalars),
        out_specs=[VMEM] * len(outs),
        scratch_shapes=list(scratch),
        compiler_params=pltpu.CompilerParams(vmem_limit_bytes=limit << 20),
        cost_estimate=pl.CostEstimate(flops=flops, bytes_accessed=4 << 20, transcendentals=0),
    )


def array(*shape, dtype=F32):
    return jax.ShapeDtypeStruct(shape, dtype)


def from_core(x):
    return lax.ppermute(x, "col", [(i, i ^ 1) for i in range(32)])


def shards(fronts, row_targets, col_targets):
    front = fronts[0]
    rows_here, cols_here = front.shape
    row = lax.axis_index("row")
    col = lax.axis_index("col")
    place = jnp.stack([row, col]).astype(jnp.int32)
    head = front[0:PIV, :]

    shares = []
    for k in range(4):
        pairs = []
        for r in range(4):
            for b in range(8):
                chip = (4 * r + SHARE_CHIP[b // 2][k]) % 16
                pairs.append((8 * r + b, 32 * r + 2 * chip + b % 2))
        shares.append(lax.ppermute(head[k * NB : (k + 1) * NB], GRID, pairs))

    corner = jnp.where(col < 2, head.reshape(4, NB, W), 0.0)
    sent = [lax.ppermute(corner[j], GRID, [(q, 32 * j + q) for q in range(2)]) for j in range(1, 4)]
    piece = jnp.where(row == 0, corner[0], (sent[0] + sent[1]) + sent[2])
    first = [lax.ppermute(piece, "col", [(q, q + 8 * j) for q in range(2)]) for j in range(1, 4)]
    shares, piece, first = lax.optimization_barrier((shares, piece, first))
    share = call(share_kernel, 4, [array(W, NB)], 1_000_000, 4)(*shares)[0]
    panel = lax.all_gather(share, "col")

    piece = piece + (first[0] + first[1]) + first[2]
    second = [
        lax.ppermute(piece, "col", [(8 * a + q, 8 * a + q + 2 * j) for a in range(4) for q in range(2)])
        for j in range(1, 4)
    ]
    piece = piece + (second[0] + second[1]) + second[2]
    half = lax.all_gather(piece, "row", tiled=True)
    head_last, row_targets, col_targets, half = lax.optimization_barrier((head, row_targets, col_targets, half))
    other = from_core(half)
    even = (col % 2) == 0
    left = jnp.where(even, half, other)
    last = jnp.where(even, other[W:PIV], half[W:PIV])
    spread = [lax.ppermute(head_last, "row", [(0, j)]) for j in range(1, 4)]

    low_a, inv_a, low_under, rest = call(
        factor_first, 3, [array(W, W)] * 4, 15_000_000_000, 12
    )(left[0:W], left[W:PIV], last)
    low_b, inv_b = call(factor_second, 1, [array(W, W)] * 2, 12_000_000_000, 12)(rest)

    inv_b, spread = lax.optimization_barrier((inv_b, spread))
    mine = jnp.where(row == 0, head, spread[0] + spread[1] + spread[2])
    z_all, top = call(solve_kernel, 7, [array(PIV, W)] * 2, 5_000_000_000, 12, scalars=1)(
        place, low_a, inv_a, low_under, low_b, inv_b, mine
    )

    local_cols = col_targets[0] - col * cols_here
    col_place = (local_cols[:, None] == jnp.arange(cols_here, dtype=jnp.int32)[None, :]).astype(jnp.bfloat16)
    targets = row_targets[0]
    live = targets >= 0
    owners = jnp.where(live, targets // 512, -1)
    hits = owners[:, None] == jnp.arange(16, dtype=jnp.int32)[None, :]
    index = jnp.arange(rows_here, dtype=jnp.int32)
    before = (index[:, None] > index[None, :]).astype(jnp.bfloat16)
    ranks = jnp.dot(before, hits.astype(jnp.bfloat16), preferred_element_type=F32)
    rank = jnp.sum(jnp.where(hits, ranks, 0.0), axis=1).astype(jnp.int32)
    slot = jnp.where(live, owners * 128 + rank, -1)
    offset = jnp.where(live, targets % 512 + 1, 0)
    digits = jnp.stack([offset // 16, offset % 16], axis=1).astype(jnp.bfloat16)
    at_slot = (index[:, None] == slot[None, :]).astype(jnp.bfloat16)
    found = jnp.dot(at_slot, digits, preferred_element_type=F32)
    offsets = (found[:, 0] * 16.0 + found[:, 1]).astype(jnp.int32) - 1
    offsets_in = lax.all_to_all(offsets.reshape(16, 1, 128), ("leaf", "row"), 0, 0, tiled=True).reshape(-1)
    select = (jnp.arange(512, dtype=jnp.int32)[:, None] == offsets_in[None, :]).astype(jnp.bfloat16)
    slot = slot.reshape(1, rows_here)
    select, slot, z_all = lax.optimization_barrier((select, slot, z_all))

    out, send = call(
        update_kernel,
        7,
        [array(rows_here, cols_here), array(2048, cols_here)],
        6_000_000_000,
        32,
        [pltpu.VMEM((rows_here, 2 * cols_here), jnp.bfloat16)],
        scalars=1,
    )(place, front, panel, z_all, top, col_place, slot)
    received = lax.all_to_all(send.reshape(16, 128, cols_here), ("leaf", "row"), 0, 0, tiled=True)
    parent = call(place_kernel, 2, [array(512, cols_here)], 1_000_000_000, 16)(
        select, received.reshape(2048, cols_here)
    )[0]
    return (out[None], parent)


def solution(mesh):
    placed = (P("leaf", "row", "col"), P("leaf", "row"), P("leaf", "col"))
    return jax.shard_map(
        shards,
        mesh=mesh,
        in_specs=placed,
        out_specs=(P("leaf", "row", "col"), P(("leaf", "row"), "col")),
        check_vma=False,
    )
```

```python
import jax
import jax.numpy as jnp
from jax import lax
from jax.experimental import pallas as pl
from jax.experimental.pallas import tpu as pltpu
from jax.sharding import PartitionSpec as P

W = 256
PIV = 512
NB = 128
HIGHEST = lax.Precision.HIGHEST
GRID = ("row", "col")
SHARE_CHIP = ((0, -1, -2, -3), (1, -4, -5, -6), (2, 7, 8, 9), (3, 4, 5, 6))

def dot_f32(a, b, dims=((1,), (0,))):
    return lax.dot_general(
        a, b, (dims, ((), ())), precision=HIGHEST, preferred_element_type=jnp.float32
    )


def split(x):
    high = x.astype(jnp.bfloat16)
    low = (x - high.astype(jnp.float32)).astype(jnp.bfloat16)
    return high, low


def factor_block(block):
    groups = NB // 8
    sub = lax.broadcasted_iota(jnp.int32, (8, NB), 0)
    lane = lax.broadcasted_iota(jnp.int32, (8, NB), 1)
    mat = [block[8 * i : 8 * i + 8, :] for i in range(groups)]
    inv = [jnp.where(lane == sub + 8 * i, 1.0, 0.0).astype(jnp.float32) for i in range(groups)]
    full = (8, NB)
    for g in range(groups):
        own = [jnp.broadcast_to(mat[g][:, 8 * g + k : 8 * g + k + 1], full) for k in range(8)]
        part = [[jnp.broadcast_to(own[b][a : a + 1, :], full) for b in range(a + 1)] for a in range(8)]
        recip, unit = [], [[None] * 8 for _ in range(8)]
        for k in range(8):
            recip.append(1.0 / part[k][k])
            for a in range(k + 1, 8):
                unit[a][k] = part[a][k] * recip[k]
            for a in range(k + 1, 8):
                for b in range(k + 1, a + 1):
                    part[a][b] = part[a][b] - unit[a][k] * part[b][k]
        row_m = [jnp.broadcast_to(mat[g][k : k + 1, :], full) for k in range(8)]
        row_i = [jnp.broadcast_to(inv[g][k : k + 1, :], full) for k in range(8)]
        for k in range(8):
            for m in range(k):
                row_m[k] = row_m[k] - unit[k][m] * row_m[m]
                row_i[k] = row_i[k] - unit[k][m] * row_i[m]
        new_m, new_i = row_m[0], row_i[0]
        for k in range(1, 8):
            new_m = jnp.where(sub == k, row_m[k], new_m)
            new_i = jnp.where(sub == k, row_i[k], new_i)
        mat[g], inv[g] = new_m, new_i
        row_m = [row_m[k] * recip[k] for k in range(8)]
        row_i = [row_i[k] * recip[k] for k in range(8)]
        for i in range(g + 1, groups):
            cols = [jnp.broadcast_to(mat[i][:, 8 * g + k : 8 * g + k + 1], full) for k in range(8)]
            for k in range(8):
                for m in range(k):
                    cols[k] = cols[k] - unit[k][m] * cols[m]
                mat[i] = mat[i] - cols[k] * row_m[k]
                inv[i] = inv[i] - cols[k] * row_i[k]
    upper, lower_inv = [], []
    for i in range(groups):
        on_diag = lane == sub + 8 * i
        diag = jnp.sum(jnp.where(on_diag, mat[i], 0.0), axis=1, keepdims=True)
        scale = 1.0 / jnp.sqrt(diag)
        upper.append(jnp.where(lane >= sub + 8 * i, mat[i] * scale, 0.0))
        lower_inv.append(inv[i] * scale)
    return jnp.concatenate(upper, axis=0), jnp.concatenate(lower_inv, axis=0)


def share_kernel(share, out_ref):
    out_ref[...] = share[...].T


def factor_two(work, low, inverse):
    first, second = slice(0, NB), slice(NB, W)
    upper, inv_a = factor_block(work[first, first])
    below = dot_f32(work[second, first], inv_a, ((1,), (1,)))
    rest = work[second, second] - dot_f32(below, below, ((1,), (1,)))
    low[first, first] = upper.T
    low[second, first] = below
    low[first, second] = jnp.zeros((NB, NB), jnp.float32)
    upper, inv_b = factor_block(rest)
    low[second, second] = upper.T
    inverse[first, first] = inv_a
    inverse[first, second] = jnp.zeros((NB, NB), jnp.float32)
    inverse[second, second] = inv_b
    inverse[second, first] = -dot_f32(inv_b, dot_f32(below, inv_a))


def factor_first(block, under, last, low, inverse, low_under, rest):
    factor_two(block, low, inverse)
    below = dot_f32(under[...], inverse[...], ((1,), (1,)))
    low_under[...] = below
    rest[...] = last[...] - dot_f32(below, below, ((1,), (1,)))


def factor_second(block, low, inverse):
    factor_two(block, low, inverse)


def solve_kernel(place, low_a, inv_a, low_under, low_b, inv_b, mine, z_ref, top_ref):
    col = place[1]
    own_a, own_b = mine[0:W, :], mine[W:PIV, :]
    solved_a = dot_f32(inv_a[...], own_a)
    second = own_b - dot_f32(low_under[...], solved_a)
    solved_b = dot_f32(inv_b[...], second)
    unit_row = lax.broadcasted_iota(jnp.int32, (W, W), 0)
    unit_col = lax.broadcasted_iota(jnp.int32, (W, W), 1)
    unit = jnp.where(unit_row == unit_col, -1.0, 0.0)
    zero = jnp.zeros((W, W), jnp.float32)
    chosen_a = jnp.where(col == 0, unit, jnp.where(col == 1, zero, solved_a))
    chosen_b = jnp.where(col == 1, unit, jnp.where(col == 0, zero, solved_b))
    z_b = dot_f32(inv_b[...], chosen_b, ((0,), (0,)))
    z_ref[W:PIV, :] = z_b
    z_ref[0:W, :] = dot_f32(inv_a[...], chosen_a - dot_f32(low_under[...], z_b, ((0,), (0,))), ((0,), (0,)))
    top_ref[0:W, :] = jnp.where(col == 0, low_a[...], jnp.where(col == 1, zero, own_a))
    top_ref[W:PIV, :] = jnp.where(col == 0, low_under[...], jnp.where(col == 1, low_b[...], second))


def update_kernel(place, front, panel, z_ref, top, col_place, slot, out_ref, send_ref, pair):
    row, col = place[0], place[1]
    keep = jnp.where(col < PIV // W, 0.0, 1.0)
    for b in range(8):
        at = slice(b * W, (b + 1) * W)
        parts = []
        for k in range(4):
            parts.append(panel[2 * ((4 * row + SHARE_CHIP[b // 2][k]) & 15) + b % 2])
        rows = jnp.concatenate(parts, axis=1)
        value = front[at, :] * keep - dot_f32(rows, z_ref[...])
        if b < PIV // W:
            value = jnp.where(row == 0, top[at, :], value)
        out_ref[at, :] = value
        for part, piece in enumerate(split(value)):
            moved = jnp.dot(piece, col_place[...], preferred_element_type=jnp.float32)
            pair[at, part * W : (part + 1) * W] = moved.astype(jnp.bfloat16)
    for b in range(4):
        want = lax.broadcasted_iota(jnp.int32, (512, 2048), 0) + b * 512
        hit = jnp.where(slot[...] == want, 1.0, 0.0).astype(jnp.bfloat16)
        both = jnp.dot(hit, pair[...], preferred_element_type=jnp.float32)
        send_ref[b * 512 : (b + 1) * 512, :] = both[:, 0:W] + both[:, W : 2 * W]


def place_kernel(select, values, out_ref):
    high, low = split(values[...])
    out_ref[...] = jnp.dot(select[...], high, preferred_element_type=jnp.float32) + jnp.dot(
        select[...], low, preferred_element_type=jnp.float32
    )


SMEM = pl.BlockSpec(memory_space=pltpu.SMEM)
VMEM = pl.BlockSpec(memory_space=pltpu.VMEM)
F32 = jnp.float32


def call(body, ins, outs, flops, limit, scratch=(), scalars=0):
    return pl.pallas_call(
        body,
        out_shape=outs,
        in_specs=[SMEM] * scalars + [VMEM] * (ins - scalars),
        out_specs=[VMEM] * len(outs),
        scratch_shapes=list(scratch),
        compiler_params=pltpu.CompilerParams(vmem_limit_bytes=limit << 20),
        cost_estimate=pl.CostEstimate(flops=flops, bytes_accessed=4 << 20, transcendentals=0),
    )


def array(*shape, dtype=F32):
    return jax.ShapeDtypeStruct(shape, dtype)


def from_core(x):
    return lax.ppermute(x, "col", [(i, i ^ 1) for i in range(32)])


def shards(fronts, row_targets, col_targets):
    front = fronts[0]
    rows_here, cols_here = front.shape
    row = lax.axis_index("row")
    col = lax.axis_index("col")
    place = jnp.stack([row, col]).astype(jnp.int32)
    head = front[0:PIV, :]

    quarter = lax.all_to_all(head.reshape(4, NB, W), "row", 0, 0, tiled=True)[0]

    local_cols = col_targets[0] - col * cols_here
    col_place = (local_cols[:, None] == jnp.arange(cols_here, dtype=jnp.int32)[None, :]).astype(jnp.bfloat16)
    targets = row_targets[0]
    live = targets >= 0
    owners = jnp.where(live, targets // 512, -1)
    hits = owners[:, None] == jnp.arange(16, dtype=jnp.int32)[None, :]
    index = jnp.arange(rows_here, dtype=jnp.int32)
    before = (index[:, None] > index[None, :]).astype(jnp.bfloat16)
    ranks = jnp.dot(before, hits.astype(jnp.bfloat16), preferred_element_type=F32)
    rank = jnp.sum(jnp.where(hits, ranks, 0.0), axis=1).astype(jnp.int32)
    slot = jnp.where(live, owners * 128 + rank, -1)
    offset = jnp.where(live, targets % 512 + 1, 0)
    digits = jnp.stack([offset // 16, offset % 16], axis=1).astype(jnp.bfloat16)
    at_slot = (index[:, None] == slot[None, :]).astype(jnp.bfloat16)
    found = jnp.dot(at_slot, digits, preferred_element_type=F32)
    offsets = (found[:, 0] * 16.0 + found[:, 1]).astype(jnp.int32) - 1
    slot = slot.reshape(1, rows_here)
    quarter, slot, offsets, col_place = lax.optimization_barrier((quarter, slot, offsets, col_place))

    pairs = []
    for k in range(4):
        for r in range(4):
            for b in range(8):
                chip = (4 * r + SHARE_CHIP[b // 2][k]) % 16
                pairs.append((32 * k + 8 * r + b, 32 * r + 2 * chip + b % 2))
    share = lax.ppermute(quarter, GRID, pairs)
    offsets_in = lax.all_to_all(offsets.reshape(16, 1, 128), ("leaf", "row"), 0, 0, tiled=True).reshape(1, 2048)
    share, quarter, head, offsets_in = lax.optimization_barrier((share, quarter, head, offsets_in))
    select = (jnp.arange(512, dtype=jnp.int32)[:, None] == offsets_in).astype(jnp.bfloat16)
    piece = jnp.where(col < 2, quarter, 0.0)
    first = [lax.ppermute(piece, "col", [(q, q + 8 * j) for q in range(2)]) for j in range(1, 4)]
    spread = [lax.ppermute(head, GRID, [(c, 32 * j + c) for c in range(2, 32)]) for j in range(1, 4)]
    panel = lax.all_gather(call(share_kernel, 1, [array(W, NB)], 1_000_000, 4)(share)[0], "col")

    piece = piece + (first[0] + first[1]) + first[2]
    second = [
        lax.ppermute(piece, "col", [(8 * a + q, 8 * a + q + 2 * j) for a in range(4) for q in range(2)])
        for j in range(1, 4)
    ]
    piece = piece + (second[0] + second[1]) + second[2]
    half = lax.all_gather(piece, "row", tiled=True)
    other = from_core(half)
    even = (col % 2) == 0
    left = jnp.where(even, half, other)
    last = jnp.where(even, other[W:PIV], half[W:PIV])

    low_a, inv_a, low_under, rest = call(
        factor_first, 3, [array(W, W)] * 4, 15_000_000_000, 12
    )(left[0:W], left[W:PIV], last)
    low_b, inv_b = call(factor_second, 1, [array(W, W)] * 2, 12_000_000_000, 12)(rest)

    inv_b, spread = lax.optimization_barrier((inv_b, spread))
    mine = jnp.where(row == 0, head, spread[0] + spread[1] + spread[2])
    z_all, top = call(solve_kernel, 7, [array(PIV, W)] * 2, 5_000_000_000, 12, scalars=1)(
        place, low_a, inv_a, low_under, low_b, inv_b, mine
    )


    select, z_all = lax.optimization_barrier((select, z_all))
    out, send = call(
        update_kernel,
        7,
        [array(rows_here, cols_here), array(2048, cols_here)],
        6_000_000_000,
        32,
        [pltpu.VMEM((rows_here, 2 * cols_here), jnp.bfloat16)],
        scalars=1,
    )(place, front, panel, z_all, top, col_place, slot)
    received = lax.all_to_all(send.reshape(16, 128, cols_here), ("leaf", "row"), 0, 0, tiled=True)
    parent = call(place_kernel, 2, [array(512, cols_here)], 1_000_000_000, 16)(
        select, received.reshape(2048, cols_here)
    )[0]
    return (out[None], parent)


def solution(mesh):
    placed = (P("leaf", "row", "col"), P("leaf", "row"), P("leaf", "col"))
    return jax.shard_map(
        shards,
        mesh=mesh,
        in_specs=placed,
        out_specs=(P("leaf", "row", "col"), P(("leaf", "row"), "col")),
        check_vma=False,
    )
```

```python
import jax
import jax.numpy as jnp
from jax import lax
from jax.experimental import pallas as pl
from jax.experimental.pallas import tpu as pltpu
from jax.sharding import PartitionSpec as P

W = 256
PIV = 512
NB = 128
HIGHEST = lax.Precision.HIGHEST
GRID = ("row", "col")
SHARE_CHIP = ((0, -1, -2, -3), (1, -4, -5, -6), (2, 7, 8, 9), (3, 4, 5, 6))

def dot_f32(a, b, dims=((1,), (0,))):
    return lax.dot_general(
        a, b, (dims, ((), ())), precision=HIGHEST, preferred_element_type=jnp.float32
    )


def split(x):
    high = x.astype(jnp.bfloat16)
    low = (x - high.astype(jnp.float32)).astype(jnp.bfloat16)
    return high, low


def factor_block(block):
    groups = NB // 8
    sub = lax.broadcasted_iota(jnp.int32, (8, NB), 0)
    lane = lax.broadcasted_iota(jnp.int32, (8, NB), 1)
    mat = [block[8 * i : 8 * i + 8, :] for i in range(groups)]
    inv = [jnp.where(lane == sub + 8 * i, 1.0, 0.0).astype(jnp.float32) for i in range(groups)]
    full = (8, NB)
    for g in range(groups):
        own = [jnp.broadcast_to(mat[g][:, 8 * g + k : 8 * g + k + 1], full) for k in range(8)]
        part = [[jnp.broadcast_to(own[b][a : a + 1, :], full) for b in range(a + 1)] for a in range(8)]
        recip, unit = [], [[None] * 8 for _ in range(8)]
        for k in range(8):
            recip.append(1.0 / part[k][k])
            for a in range(k + 1, 8):
                unit[a][k] = part[a][k] * recip[k]
            for a in range(k + 1, 8):
                for b in range(k + 1, a + 1):
                    part[a][b] = part[a][b] - unit[a][k] * part[b][k]
        row_m = [jnp.broadcast_to(mat[g][k : k + 1, :], full) for k in range(8)]
        row_i = [jnp.broadcast_to(inv[g][k : k + 1, :], full) for k in range(8)]
        for k in range(8):
            for m in range(k):
                row_m[k] = row_m[k] - unit[k][m] * row_m[m]
                row_i[k] = row_i[k] - unit[k][m] * row_i[m]
        new_m, new_i = row_m[0], row_i[0]
        for k in range(1, 8):
            new_m = jnp.where(sub == k, row_m[k], new_m)
            new_i = jnp.where(sub == k, row_i[k], new_i)
        mat[g], inv[g] = new_m, new_i
        row_m = [row_m[k] * recip[k] for k in range(8)]
        row_i = [row_i[k] * recip[k] for k in range(8)]
        for i in range(g + 1, groups):
            cols = [jnp.broadcast_to(mat[i][:, 8 * g + k : 8 * g + k + 1], full) for k in range(8)]
            for k in range(8):
                for m in range(k):
                    cols[k] = cols[k] - unit[k][m] * cols[m]
                mat[i] = mat[i] - cols[k] * row_m[k]
                inv[i] = inv[i] - cols[k] * row_i[k]
    upper, lower_inv = [], []
    for i in range(groups):
        on_diag = lane == sub + 8 * i
        diag = jnp.sum(jnp.where(on_diag, mat[i], 0.0), axis=1, keepdims=True)
        scale = 1.0 / jnp.sqrt(diag)
        upper.append(jnp.where(lane >= sub + 8 * i, mat[i] * scale, 0.0))
        lower_inv.append(inv[i] * scale)
    return jnp.concatenate(upper, axis=0), jnp.concatenate(lower_inv, axis=0)


def share_kernel(share, out_ref):
    out_ref[...] = share[...].T


def factor_two(work, low, inverse):
    first, second = slice(0, NB), slice(NB, W)
    upper, inv_a = factor_block(work[first, first])
    below = dot_f32(work[second, first], inv_a, ((1,), (1,)))
    rest = work[second, second] - dot_f32(below, below, ((1,), (1,)))
    low[first, first] = upper.T
    low[second, first] = below
    low[first, second] = jnp.zeros((NB, NB), jnp.float32)
    upper, inv_b = factor_block(rest)
    low[second, second] = upper.T
    inverse[first, first] = inv_a
    inverse[first, second] = jnp.zeros((NB, NB), jnp.float32)
    inverse[second, second] = inv_b
    inverse[second, first] = -dot_f32(inv_b, dot_f32(below, inv_a))


def factor_first(block, under, last, low, inverse, low_under, rest):
    factor_two(block, low, inverse)
    below = dot_f32(under[...], inverse[...], ((1,), (1,)))
    low_under[...] = below
    rest[...] = last[...] - dot_f32(below, below, ((1,), (1,)))


def factor_second(block, low, inverse):
    factor_two(block, low, inverse)


def solve_kernel(place, low_a, inv_a, low_under, low_b, inv_b, mine, z_ref, top_ref):
    col = place[1]
    own_a, own_b = mine[0:W, :], mine[W:PIV, :]
    solved_a = dot_f32(inv_a[...], own_a)
    second = own_b - dot_f32(low_under[...], solved_a)
    solved_b = dot_f32(inv_b[...], second)
    unit_row = lax.broadcasted_iota(jnp.int32, (W, W), 0)
    unit_col = lax.broadcasted_iota(jnp.int32, (W, W), 1)
    unit = jnp.where(unit_row == unit_col, -1.0, 0.0)
    zero = jnp.zeros((W, W), jnp.float32)
    chosen_a = jnp.where(col == 0, unit, jnp.where(col == 1, zero, solved_a))
    chosen_b = jnp.where(col == 1, unit, jnp.where(col == 0, zero, solved_b))
    z_b = dot_f32(inv_b[...], chosen_b, ((0,), (0,)))
    z_ref[W:PIV, :] = z_b
    z_ref[0:W, :] = dot_f32(inv_a[...], chosen_a - dot_f32(low_under[...], z_b, ((0,), (0,))), ((0,), (0,)))
    top_ref[0:W, :] = jnp.where(col == 0, low_a[...], jnp.where(col == 1, zero, own_a))
    top_ref[W:PIV, :] = jnp.where(col == 0, low_under[...], jnp.where(col == 1, low_b[...], second))


def update_kernel(place, front, panel, z_ref, top, col_place, slot, out_ref, send_ref, pair):
    row, col = place[0], place[1]
    keep = jnp.where(col < PIV // W, 0.0, 1.0)
    for b in range(8):
        at = slice(b * W, (b + 1) * W)
        parts = []
        for k in range(4):
            parts.append(panel[2 * ((4 * row + SHARE_CHIP[b // 2][k]) & 15) + b % 2])
        rows = jnp.concatenate(parts, axis=1)
        value = front[at, :] * keep - dot_f32(rows, z_ref[...])
        if b < PIV // W:
            value = jnp.where(row == 0, top[at, :], value)
        out_ref[at, :] = value
        for part, piece in enumerate(split(value)):
            moved = jnp.dot(piece, col_place[...], preferred_element_type=jnp.float32)
            pair[at, part * W : (part + 1) * W] = moved.astype(jnp.bfloat16)
    for b in range(4):
        want = lax.broadcasted_iota(jnp.int32, (512, 2048), 0) + b * 512
        hit = jnp.where(slot[...] == want, 1.0, 0.0).astype(jnp.bfloat16)
        both = jnp.dot(hit, pair[...], preferred_element_type=jnp.float32)
        send_ref[b * 512 : (b + 1) * 512, :] = both[:, 0:W] + both[:, W : 2 * W]


def place_kernel(select, values, out_ref):
    high, low = split(values[...])
    out_ref[...] = jnp.dot(select[...], high, preferred_element_type=jnp.float32) + jnp.dot(
        select[...], low, preferred_element_type=jnp.float32
    )


SMEM = pl.BlockSpec(memory_space=pltpu.SMEM)
VMEM = pl.BlockSpec(memory_space=pltpu.VMEM)
F32 = jnp.float32


def call(body, ins, outs, flops, limit, scratch=(), scalars=0):
    return pl.pallas_call(
        body,
        out_shape=outs,
        in_specs=[SMEM] * scalars + [VMEM] * (ins - scalars),
        out_specs=[VMEM] * len(outs),
        scratch_shapes=list(scratch),
        compiler_params=pltpu.CompilerParams(vmem_limit_bytes=limit << 20),
        cost_estimate=pl.CostEstimate(flops=flops, bytes_accessed=4 << 20, transcendentals=0),
    )


def array(*shape, dtype=F32):
    return jax.ShapeDtypeStruct(shape, dtype)


def from_core(x):
    return lax.ppermute(x, "col", [(i, i ^ 1) for i in range(32)])


def shards(fronts, row_targets, col_targets):
    front = fronts[0]
    rows_here, cols_here = front.shape
    row = lax.axis_index("row")
    col = lax.axis_index("col")
    place = jnp.stack([row, col]).astype(jnp.int32)
    head = front[0:PIV, :]

    quarter = lax.all_to_all(head.reshape(4, NB, W), "row", 0, 0, tiled=True)[0]

    local_cols = col_targets[0] - col * cols_here
    col_place = (local_cols[:, None] == jnp.arange(cols_here, dtype=jnp.int32)[None, :]).astype(jnp.bfloat16)
    targets = row_targets[0]
    live = targets >= 0
    owners = jnp.where(live, targets // 512, -1)
    hits = owners[:, None] == jnp.arange(16, dtype=jnp.int32)[None, :]
    index = jnp.arange(rows_here, dtype=jnp.int32)
    before = (index[:, None] > index[None, :]).astype(jnp.bfloat16)
    ranks = jnp.dot(before, hits.astype(jnp.bfloat16), preferred_element_type=F32)
    rank = jnp.sum(jnp.where(hits, ranks, 0.0), axis=1).astype(jnp.int32)
    slot = jnp.where(live, owners * 128 + rank, -1)
    offset = jnp.where(live, targets % 512 + 1, 0)
    digits = jnp.stack([offset // 16, offset % 16], axis=1).astype(jnp.bfloat16)
    at_slot = (index[:, None] == slot[None, :]).astype(jnp.bfloat16)
    found = jnp.dot(at_slot, digits, preferred_element_type=F32)
    offsets = (found[:, 0] * 16.0 + found[:, 1]).astype(jnp.int32) - 1
    slot = slot.reshape(1, rows_here)
    quarter, slot, offsets, col_place = lax.optimization_barrier((quarter, slot, offsets, col_place))

    pairs = []
    for k in range(4):
        for r in range(4):
            for b in range(8):
                chip = (4 * r + SHARE_CHIP[b // 2][k]) % 16
                pairs.append((32 * k + 8 * r + b, 32 * r + 2 * chip + b % 2))
    share = lax.ppermute(quarter, GRID, pairs)
    offsets_in = lax.all_to_all(offsets.reshape(16, 1, 128), ("leaf", "row"), 0, 0, tiled=True).reshape(1, 2048)
    share, quarter, head, offsets_in = lax.optimization_barrier((share, quarter, head, offsets_in))
    select = (jnp.arange(512, dtype=jnp.int32)[:, None] == offsets_in).astype(jnp.bfloat16)
    piece = jnp.where(col < 2, quarter, 0.0)
    lanes = [(r, q) for r in range(4) for q in range(2) if q == 0 or r >= 2]
    first = [lax.ppermute(piece, GRID, [(32 * r + q, 32 * r + q + 8 * j) for r, q in lanes]) for j in range(1, 4)]
    spread = [lax.ppermute(head, GRID, [(c, 32 * j + c) for c in range(2, 32)]) for j in range(1, 4)]
    panel = lax.all_gather(call(share_kernel, 1, [array(W, NB)], 1_000_000, 4)(share)[0], "col")

    piece = piece + (first[0] + first[1]) + first[2]
    second = [
        lax.ppermute(
            piece, GRID, [(32 * r + 8 * a + q, 32 * r + 8 * a + q + 2 * j) for r, q in lanes for a in range(4)]
        )
        for j in range(1, 4)
    ]
    piece = piece + (second[0] + second[1]) + second[2]
    half = lax.all_gather(piece, "row", tiled=True)
    other = from_core(half)
    even = (col % 2) == 0
    left = jnp.where(even, half, other)
    last = jnp.where(even, other[W:PIV], half[W:PIV])

    low_a, inv_a, low_under, rest = call(
        factor_first, 3, [array(W, W)] * 4, 15_000_000_000, 12
    )(left[0:W], left[W:PIV], last)
    low_b, inv_b = call(factor_second, 1, [array(W, W)] * 2, 12_000_000_000, 12)(rest)

    inv_b, spread = lax.optimization_barrier((inv_b, spread))
    mine = jnp.where(row == 0, head, spread[0] + spread[1] + spread[2])
    z_all, top = call(solve_kernel, 7, [array(PIV, W)] * 2, 5_000_000_000, 12, scalars=1)(
        place, low_a, inv_a, low_under, low_b, inv_b, mine
    )


    select, z_all = lax.optimization_barrier((select, z_all))
    out, send = call(
        update_kernel,
        7,
        [array(rows_here, cols_here), array(2048, cols_here)],
        6_000_000_000,
        32,
        [pltpu.VMEM((rows_here, 2 * cols_here), jnp.bfloat16)],
        scalars=1,
    )(place, front, panel, z_all, top, col_place, slot)
    received = lax.all_to_all(send.reshape(16, 128, cols_here), ("leaf", "row"), 0, 0, tiled=True)
    parent = call(place_kernel, 2, [array(512, cols_here)], 1_000_000_000, 16)(
        select, received.reshape(2048, cols_here)
    )[0]
    return (out[None], parent)


def solution(mesh):
    placed = (P("leaf", "row", "col"), P("leaf", "row"), P("leaf", "col"))
    return jax.shard_map(
        shards,
        mesh=mesh,
        in_specs=placed,
        out_specs=(P("leaf", "row", "col"), P(("leaf", "row"), "col")),
        check_vma=False,
    )
```

```python
import jax
import jax.numpy as jnp
from jax import lax
from jax.experimental import pallas as pl
from jax.experimental.pallas import tpu as pltpu
from jax.sharding import PartitionSpec as P

W = 256
PIV = 512
NB = 128
HIGHEST = lax.Precision.HIGHEST
GRID = ("row", "col")
SHARE_CHIP = ((0, -1, -2, -3), (1, -4, -5, -6), (2, 7, 8, 9), (3, 4, 5, 6))

def dot_f32(a, b, dims=((1,), (0,))):
    return lax.dot_general(
        a, b, (dims, ((), ())), precision=HIGHEST, preferred_element_type=jnp.float32
    )


def split(x):
    high = x.astype(jnp.bfloat16)
    low = (x - high.astype(jnp.float32)).astype(jnp.bfloat16)
    return high, low


def factor_block(block):
    groups = NB // 8
    sub = lax.broadcasted_iota(jnp.int32, (8, NB), 0)
    lane = lax.broadcasted_iota(jnp.int32, (8, NB), 1)
    mat = [block[8 * i : 8 * i + 8, :] for i in range(groups)]
    inv = [jnp.where(lane == sub + 8 * i, 1.0, 0.0).astype(jnp.float32) for i in range(groups)]
    full = (8, NB)
    for g in range(groups):
        own = [jnp.broadcast_to(mat[g][:, 8 * g + k : 8 * g + k + 1], full) for k in range(8)]
        part = [[jnp.broadcast_to(own[b][a : a + 1, :], full) for b in range(a + 1)] for a in range(8)]
        recip, unit = [], [[None] * 8 for _ in range(8)]
        for k in range(8):
            recip.append(1.0 / part[k][k])
            for a in range(k + 1, 8):
                unit[a][k] = part[a][k] * recip[k]
            for a in range(k + 1, 8):
                for b in range(k + 1, a + 1):
                    part[a][b] = part[a][b] - unit[a][k] * part[b][k]
        row_m = [jnp.broadcast_to(mat[g][k : k + 1, :], full) for k in range(8)]
        row_i = [jnp.broadcast_to(inv[g][k : k + 1, :], full) for k in range(8)]
        for k in range(8):
            for m in range(k):
                row_m[k] = row_m[k] - unit[k][m] * row_m[m]
                row_i[k] = row_i[k] - unit[k][m] * row_i[m]
        new_m, new_i = row_m[0], row_i[0]
        for k in range(1, 8):
            new_m = jnp.where(sub == k, row_m[k], new_m)
            new_i = jnp.where(sub == k, row_i[k], new_i)
        mat[g], inv[g] = new_m, new_i
        row_m = [row_m[k] * recip[k] for k in range(8)]
        row_i = [row_i[k] * recip[k] for k in range(8)]
        for i in range(g + 1, groups):
            cols = [jnp.broadcast_to(mat[i][:, 8 * g + k : 8 * g + k + 1], full) for k in range(8)]
            for k in range(8):
                for m in range(k):
                    cols[k] = cols[k] - unit[k][m] * cols[m]
                mat[i] = mat[i] - cols[k] * row_m[k]
                inv[i] = inv[i] - cols[k] * row_i[k]
    upper, lower_inv = [], []
    for i in range(groups):
        on_diag = lane == sub + 8 * i
        diag = jnp.sum(jnp.where(on_diag, mat[i], 0.0), axis=1, keepdims=True)
        scale = 1.0 / jnp.sqrt(diag)
        upper.append(jnp.where(lane >= sub + 8 * i, mat[i] * scale, 0.0))
        lower_inv.append(inv[i] * scale)
    return jnp.concatenate(upper, axis=0), jnp.concatenate(lower_inv, axis=0)


def share_kernel(share, out_ref):
    out_ref[...] = share[...].T


def factor_two(work, low, inverse):
    first, second = slice(0, NB), slice(NB, W)
    upper, inv_a = factor_block(work[first, first])
    below = dot_f32(work[second, first], inv_a, ((1,), (1,)))
    rest = work[second, second] - dot_f32(below, below, ((1,), (1,)))
    low[first, first] = upper.T
    low[second, first] = below
    low[first, second] = jnp.zeros((NB, NB), jnp.float32)
    upper, inv_b = factor_block(rest)
    low[second, second] = upper.T
    inverse[first, first] = inv_a
    inverse[first, second] = jnp.zeros((NB, NB), jnp.float32)
    inverse[second, second] = inv_b
    inverse[second, first] = -dot_f32(inv_b, dot_f32(below, inv_a))


def factor_first(block, under, last, low, inverse, low_under, rest):
    factor_two(block, low, inverse)
    below = dot_f32(under[...], inverse[...], ((1,), (1,)))
    low_under[...] = below
    rest[...] = last[...] - dot_f32(below, below, ((1,), (1,)))


def factor_second(block, low, inverse):
    factor_two(block, low, inverse)


def solve_kernel(place, low_a, inv_a, low_under, low_b, inv_b, mine, z_ref, top_ref):
    col = place[1]
    own_a, own_b = mine[0:W, :], mine[W:PIV, :]
    solved_a = dot_f32(inv_a[...], own_a)
    second = own_b - dot_f32(low_under[...], solved_a)
    solved_b = dot_f32(inv_b[...], second)
    unit_row = lax.broadcasted_iota(jnp.int32, (W, W), 0)
    unit_col = lax.broadcasted_iota(jnp.int32, (W, W), 1)
    unit = jnp.where(unit_row == unit_col, -1.0, 0.0)
    zero = jnp.zeros((W, W), jnp.float32)
    chosen_a = jnp.where(col == 0, unit, jnp.where(col == 1, zero, solved_a))
    chosen_b = jnp.where(col == 1, unit, jnp.where(col == 0, zero, solved_b))
    z_b = dot_f32(inv_b[...], chosen_b, ((0,), (0,)))
    z_ref[W:PIV, :] = z_b
    z_ref[0:W, :] = dot_f32(inv_a[...], chosen_a - dot_f32(low_under[...], z_b, ((0,), (0,))), ((0,), (0,)))
    top_ref[0:W, :] = jnp.where(col == 0, low_a[...], jnp.where(col == 1, zero, own_a))
    top_ref[W:PIV, :] = jnp.where(col == 0, low_under[...], jnp.where(col == 1, low_b[...], second))


def update_kernel(place, front, panel, z_ref, top, col_place, slot, out_ref, send_ref, pair):
    row, col = place[0], place[1]
    keep = jnp.where(col < PIV // W, 0.0, 1.0)
    for b in range(8):
        at = slice(b * W, (b + 1) * W)
        parts = []
        for k in range(4):
            parts.append(panel[2 * ((4 * row + SHARE_CHIP[b // 2][k]) & 15) + b % 2])
        rows = jnp.concatenate(parts, axis=1)
        value = front[at, :] * keep - dot_f32(rows, z_ref[...])
        if b < PIV // W:
            value = jnp.where(row == 0, top[at, :], value)
        out_ref[at, :] = value
        for part, piece in enumerate(split(value)):
            moved = jnp.dot(piece, col_place[...], preferred_element_type=jnp.float32)
            pair[at, part * W : (part + 1) * W] = moved.astype(jnp.bfloat16)
    for b in range(4):
        want = lax.broadcasted_iota(jnp.int32, (512, 2048), 0) + b * 512
        hit = jnp.where(slot[...] == want, 1.0, 0.0).astype(jnp.bfloat16)
        both = jnp.dot(hit, pair[...], preferred_element_type=jnp.float32)
        send_ref[b * 512 : (b + 1) * 512, :] = both[:, 0:W] + both[:, W : 2 * W]


def place_kernel(select, values, out_ref):
    high, low = split(values[...])
    out_ref[...] = jnp.dot(select[...], high, preferred_element_type=jnp.float32) + jnp.dot(
        select[...], low, preferred_element_type=jnp.float32
    )


SMEM = pl.BlockSpec(memory_space=pltpu.SMEM)
VMEM = pl.BlockSpec(memory_space=pltpu.VMEM)
F32 = jnp.float32


def call(body, ins, outs, flops, limit, scratch=(), scalars=0):
    return pl.pallas_call(
        body,
        out_shape=outs,
        in_specs=[SMEM] * scalars + [VMEM] * (ins - scalars),
        out_specs=[VMEM] * len(outs),
        scratch_shapes=list(scratch),
        compiler_params=pltpu.CompilerParams(vmem_limit_bytes=limit << 20),
        cost_estimate=pl.CostEstimate(flops=flops, bytes_accessed=4 << 20, transcendentals=0),
    )


def array(*shape, dtype=F32):
    return jax.ShapeDtypeStruct(shape, dtype)


def from_core(x):
    return lax.ppermute(x, "col", [(i, i ^ 1) for i in range(32)])


def shards(fronts, row_targets, col_targets):
    front = fronts[0]
    rows_here, cols_here = front.shape
    row = lax.axis_index("row")
    col = lax.axis_index("col")
    place = jnp.stack([row, col]).astype(jnp.int32)
    head = front[0:PIV, :]

    quarter = lax.all_to_all(head.reshape(4, NB, W), "row", 0, 0, tiled=True)[0]

    local_cols = col_targets[0] - col * cols_here
    col_place = (local_cols[:, None] == jnp.arange(cols_here, dtype=jnp.int32)[None, :]).astype(jnp.bfloat16)
    targets = row_targets[0]
    live = targets >= 0
    owners = jnp.where(live, targets // 512, -1)
    hits = owners[:, None] == jnp.arange(16, dtype=jnp.int32)[None, :]
    index = jnp.arange(rows_here, dtype=jnp.int32)
    before = (index[:, None] > index[None, :]).astype(jnp.bfloat16)
    ranks = jnp.dot(before, hits.astype(jnp.bfloat16), preferred_element_type=F32)
    rank = jnp.sum(jnp.where(hits, ranks, 0.0), axis=1).astype(jnp.int32)
    slot = jnp.where(live, owners * 128 + rank, -1)
    offset = jnp.where(live, targets % 512 + 1, 0)
    digits = jnp.stack([offset // 16, offset % 16], axis=1).astype(jnp.bfloat16)
    at_slot = (index[:, None] == slot[None, :]).astype(jnp.bfloat16)
    found = jnp.dot(at_slot, digits, preferred_element_type=F32)
    offsets = (found[:, 0] * 16.0 + found[:, 1]).astype(jnp.int32) - 1
    slot = slot.reshape(1, rows_here)
    quarter, slot, offsets, col_place = lax.optimization_barrier((quarter, slot, offsets, col_place))

    pairs = []
    for k in range(4):
        for r in range(4):
            for b in range(8):
                chip = (4 * r + SHARE_CHIP[b // 2][k]) % 16
                pairs.append((32 * k + 8 * r + b, 32 * r + 2 * chip + b % 2))
    share = lax.ppermute(quarter, GRID, pairs)
    offsets_in = lax.all_to_all(offsets.reshape(16, 1, 128), ("leaf", "row"), 0, 0, tiled=True).reshape(1, 2048)
    share, quarter, head, offsets_in = lax.optimization_barrier((share, quarter, head, offsets_in))
    select = (jnp.arange(512, dtype=jnp.int32)[:, None] == offsets_in).astype(jnp.bfloat16)
    piece = jnp.where(col < 2, quarter, 0.0)
    lanes = [(r, q) for r in range(4) for q in range(2) if q == 0 or r >= 2]
    first = [lax.ppermute(piece, GRID, [(32 * r + q, 32 * r + q + 8 * j) for r, q in lanes]) for j in range(1, 4)]
    spread = [lax.ppermute(head, GRID, [(c, 32 * j + c) for c in range(2, 32)]) for j in range(1, 4)]
    panel = lax.all_gather(call(share_kernel, 1, [array(W, NB)], 1_000_000, 4)(share)[0], "col")

    piece = piece + (first[0] + first[1]) + first[2]
    second = [
        lax.ppermute(
            piece, GRID, [(32 * r + 8 * a + q, 32 * r + 8 * a + q + 2 * j) for r, q in lanes for a in range(4)]
        )
        for j in range(1, 4)
    ]
    piece = piece + (second[0] + second[1]) + second[2]
    half = lax.all_gather(piece, "row", tiled=True)
    other = from_core(half)
    even = (col % 2) == 0
    left = jnp.where(even, half, other)
    last = jnp.where(even, other[W:PIV], half[W:PIV])

    low_a, inv_a, low_under, rest = call(
        factor_first, 3, [array(W, W)] * 4, 15_000_000_000, 12
    )(left[0:W], left[W:PIV], last)
    low_b, inv_b = call(factor_second, 1, [array(W, W)] * 2, 12_000_000_000, 12)(rest)

    inv_b, spread = lax.optimization_barrier((inv_b, spread))
    mine = jnp.where(row == 0, head, spread[0] + spread[1] + spread[2])
    z_all, top = call(solve_kernel, 7, [array(PIV, W)] * 2, 5_000_000_000, 12, scalars=1)(
        place, low_a, inv_a, low_under, low_b, inv_b, mine
    )


    select, z_all = lax.optimization_barrier((select, z_all))
    out, send = call(
        update_kernel,
        7,
        [array(rows_here, cols_here), array(2048, cols_here)],
        6_000_000_000,
        52,
        [pltpu.VMEM((rows_here, 2 * cols_here), jnp.bfloat16)],
        scalars=1,
    )(place, front, panel, z_all, top, col_place, slot)
    received = lax.all_to_all(send.reshape(16, 128, cols_here), ("leaf", "row"), 0, 0, tiled=True)
    parent = call(place_kernel, 2, [array(512, cols_here)], 1_000_000_000, 16)(
        select, received.reshape(2048, cols_here)
    )[0]
    return (out[None], parent)


def solution(mesh):
    placed = (P("leaf", "row", "col"), P("leaf", "row"), P("leaf", "col"))
    return jax.shard_map(
        shards,
        mesh=mesh,
        in_specs=placed,
        out_specs=(P("leaf", "row", "col"), P(("leaf", "row"), "col")),
        check_vma=False,
    )
```
